32 devices in a mesh: dp: 8 (over z, y), seq: 4 (over x, core).
Axes of the slice: x: 2, y: 2, z: 4, core: 2. Of those that a mesh axis runs over, the one named last changes fastest.
Arguments:
- tokens: bfloat16 [16, 1024, 768], P('dp', 'seq'), may hold values from -6 to 6
- lengths: int32 [16], P('dp'), may hold values from 128 to 1024, as said below
- entry_gain: bfloat16 [768], P(('dp', 'seq')), may hold values from 0.5 to 1.5
- entry_shift: bfloat16 [768], P(('dp', 'seq')), may hold values from -1 to 1
- joined_weight: bfloat16 [768, 2304], P(('dp', 'seq')), may hold values from -0.3125 to 0.3125
- joined_bias: bfloat16 [1536], P(('dp', 'seq')), may hold values from -1 to 1
- mixer_weight: bfloat16 [768, 768], P(('dp', 'seq')), may hold values from -1.25 to 1.25
- mixer_bias: bfloat16 [768], P(('dp', 'seq')), may hold values from -1 to 1
- middle_gain: bfloat16 [768], P(('dp', 'seq')), may hold values from 0.5 to 1.5
- middle_shift: bfloat16 [768], P(('dp', 'seq')), may hold values from -1 to 1
- widen_weight: bfloat16 [768, 3072], P(('dp', 'seq')), may hold values from -0.21875 to 0.21875
- widen_bias: bfloat16 [3072], P(('dp', 'seq')), may hold values from -1 to 1
- narrow_weight: bfloat16 [3072, 768], P(('dp', 'seq')), may hold values from -0.109375 to 0.109375
- narrow_bias: bfloat16 [768], P(('dp', 'seq')), may hold values from -1 to 1
- cotangent: bfloat16 [16, 1024, 768], P('dp', 'seq'), may hold values from -6 to 6
Outputs:
- mixed_out: bfloat16 [16, 1024, 768], P('dp', 'seq')
- tokens_grad: bfloat16 [16, 1024, 768], P('dp', 'seq')
- entry_gain_grad: float32 [768], P(('dp', 'seq'))
- entry_shift_grad: float32 [768], P(('dp', 'seq'))
- joined_weight_grad: float32 [768, 2304], P(('dp', 'seq'))
- joined_bias_grad: float32 [1536], P(('dp', 'seq'))
- mixer_weight_grad: float32 [768, 768], P(('dp', 'seq'))
- mixer_bias_grad: float32 [768], P(('dp', 'seq'))
- middle_gain_grad: float32 [768], P(('dp', 'seq'))
- middle_shift_grad: float32 [768], P(('dp', 'seq'))
- widen_weight_grad: float32 [768, 3072], P(('dp', 'seq'))
- widen_bias_grad: float32 [3072], P(('dp', 'seq'))
- narrow_weight_grad: float32 [3072, 768], P(('dp', 'seq'))
- narrow_bias_grad: float32 [768], P(('dp', 'seq'))
The draws below stay inside these ranges and needn't reach their ends.
Inputs may be any that keep to these rules, and one draw needn't show every extreme that they name: `lengths`: some sequence holds all 1024 slots as true tokens.
All inputs are finite; a program needn't handle non-finite values.
Results may differ from the reference program's by a relative error of at most 0.024.
The reference program's roundings to bfloat16 on the way count: a program that leaves them out, or rounds other values in their place, can miss the bound.
Values may be sent and summed in bfloat16 or wider, within the bound.
No kernel may reach another device: no remote copies, remote signals or barrier semaphores. Data moves between devices by JAX's collectives and lax.ppermute only.
A program may use at most 192 MiB of HBM per device.

```python
import jax
import jax.numpy as jnp
from jax import lax

D = 768
H = 12
FF = 3072
HD = 64
SEQ = 1024
MINLEN = 128
LAYERS = 2
SEQS_DEV = 2
BATCH = 16


def draw_lengths(key, part):
    first_key = jax.random.fold_in(key, 11)
    second_key = jax.random.fold_in(key, 23)
    drawn = jax.random.randint(first_key, (BATCH,), MINLEN, SEQ + 1, dtype=jnp.int32)
    chosen = jax.random.randint(second_key, (), 0, BATCH, dtype=jnp.int32)
    return jnp.where(jnp.arange(BATCH, dtype=jnp.int32) == chosen, SEQ, drawn).astype(jnp.int32)


def levels(key, dims, split, least, top_value):
    level, own = 1.0, jax.random.fold_in(key, 6)
    for position, parts in split:
        steps = jnp.exp(jax.random.uniform(jax.random.fold_in(own, position), (parts,), jnp.float32, least / len(split), top_value / len(split)))
        level = level * jnp.repeat(steps, dims[position] // parts).reshape([-1 if axis == position else 1 for axis in range(len(dims))])
    return level


def scatter_about(stream_key, shape, width, limit, cuts=(), kind=jnp.bfloat16):
    loudness = levels(stream_key, shape, cuts, -0.22, 0.18) if cuts else 1.0
    array = jax.random.normal(stream_key, shape, jnp.float32) * width * loudness
    return jnp.minimum(jnp.maximum(array, -limit), limit).astype(kind)


def setup_inputs(seed: int = 0) -> dict:
    streams_of = jax.random.split(jax.random.key(seed), 16)
    tokens = scatter_about(streams_of[0], (BATCH, SEQ, D), 1.0, 6.0, ((0, 8), (1, 4)))
    lengths = draw_lengths(jax.random.fold_in(streams_of[15], 71), 0)
    entry_gain = jnp.clip(1.0 + 0.1 * jax.random.normal(streams_of[2], (D,), jnp.float32), 0.5, 1.5).astype(jnp.bfloat16)
    entry_shift = scatter_about(streams_of[3], (D,), 0.2, 1.0, ((0, 32),))
    joined_weight = scatter_about(streams_of[4], (D, 3 * D), (D // 2) ** -0.5, 0.3125, ((0, 32),))
    joined_bias = scatter_about(streams_of[5], (2 * D,), 0.2, 1.0, ((0, 32),))
    mixer_weight = scatter_about(streams_of[6], (D, D), (D // 32) ** -0.5, 1.25, ((0, 32),))
    mixer_bias = scatter_about(streams_of[7], (D,), 0.2, 1.0, ((0, 32),))
    middle_gain = jnp.clip(1.0 + 0.1 * jax.random.normal(streams_of[8], (D,), jnp.float32), 0.5, 1.5).astype(jnp.bfloat16)
    middle_shift = scatter_about(streams_of[9], (D,), 0.2, 1.0, ((0, 32),))
    widen_weight = scatter_about(streams_of[10], (D, FF), D ** -0.5, 0.21875, ((0, 32),))
    widen_bias = scatter_about(streams_of[11], (FF,), 0.2, 1.0, ((0, 32),))
    narrow_weight = scatter_about(streams_of[12], (FF, D), FF ** -0.5, 0.109375, ((0, 32),))
    narrow_bias = scatter_about(streams_of[13], (D,), 0.2, 1.0, ((0, 32),))
    cotangent = scatter_about(streams_of[14], (BATCH, SEQ, D), 1.0, 6.0, ((0, 8), (1, 4)))
    return dict(tokens=tokens, lengths=lengths, entry_gain=entry_gain, entry_shift=entry_shift, joined_weight=joined_weight, joined_bias=joined_bias, mixer_weight=mixer_weight, mixer_bias=mixer_bias, middle_gain=middle_gain, middle_shift=middle_shift, widen_weight=widen_weight, widen_bias=widen_bias, narrow_weight=narrow_weight, narrow_bias=narrow_bias, cotangent=cotangent)


@jax.custom_vjp
def low(v):
    return lax.optimization_barrier(v.astype(jnp.bfloat16)).astype(jnp.float32)

@jax.custom_vjp
def low_back(v):
    return v

def low_keep(v):
    return (low(v), None)

def low_pass(kept, grad):
    return (grad,)

def back_keep(v):
    return (v, None)

def back_low(kept, grad):
    return (low(grad),)
low.defvjp(low_keep, low_pass)
low_back.defvjp(back_keep, back_low)
EPSILON = 1e-05
NEGATIVE = -1e+30
HIGHEST = lax.Precision.HIGHEST

def layer_norm(inputs, gain_row, shift_row):
    center = lax.optimization_barrier(jnp.mean(inputs, axis=-1, keepdims=True))
    offset = inputs - center
    spread = lax.optimization_barrier(jnp.mean(offset * offset, axis=-1, keepdims=True))
    return offset * lax.rsqrt(spread + EPSILON) * gain_row + shift_row

def attend_item(packet):
    queries, key_rows, values, length = packet
    places = jnp.arange(queries.shape[0], dtype=jnp.int32)
    scaling = queries.shape[1] ** (-0.5)
    scores = low_back(jnp.dot(queries, key_rows.T, precision=HIGHEST) * scaling)
    allowed = (places[None, :] <= places[:, None]) & (places[None, :] < length)
    masked = jnp.where(allowed, scores, NEGATIVE)
    row_top = lax.optimization_barrier(jnp.max(masked, axis=1, keepdims=True))
    lifted = jnp.exp(masked - row_top)
    shares = lifted / lax.optimization_barrier(jnp.sum(lifted, axis=1, keepdims=True))
    return jnp.dot(low(shares), values, precision=HIGHEST)

def split_heads(packed):
    groups = packed.shape[0]
    return packed.reshape(groups, SEQ, H, HD).transpose(0, 2, 1, 3).reshape(groups * H, SEQ, HD)

def merge_heads(items, groups):
    return items.reshape(groups, H, SEQ, HD).transpose(0, 2, 1, 3).reshape(groups, SEQ, D)

def residual_block(params, stream, lengths):
    entry_gain, entry_shift, joined_weight, joined_bias, mixer_weight, mixer_bias, middle_gain, middle_shift, widen_weight, widen_bias, narrow_weight, narrow_bias = params
    groups = stream.shape[0]
    normed = low(layer_norm(stream, entry_gain, entry_shift))
    bias_row = jnp.concatenate([joined_bias[:D], jnp.zeros_like(joined_bias[:D]), joined_bias[D:]])
    joined_rows = jnp.einsum('gtd,de->gte', normed, joined_weight, precision=HIGHEST) + bias_row
    queries = low_back(low(joined_rows[..., :D]))
    key_rows = low_back(low(joined_rows[..., D:2 * D]))
    values = low_back(low(joined_rows[..., 2 * D:]))
    item_lengths = jnp.repeat(lengths, H)
    mixed_rows = lax.map(jax.checkpoint(attend_item), (split_heads(queries), split_heads(key_rows), split_heads(values), item_lengths))
    mixed_rows = low_back(low(merge_heads(mixed_rows, groups)))
    middle = stream + low_back(jnp.einsum('gtd,de->gte', mixed_rows, mixer_weight, precision=HIGHEST) + mixer_bias)
    normed_two = low(layer_norm(middle, middle_gain, middle_shift))
    widened = low_back(jnp.einsum('gtd,df->gtf', normed_two, widen_weight, precision=HIGHEST) + widen_bias)
    activated = low(jax.nn.gelu(widened, approximate=True))
    return middle + low_back(jnp.einsum('gtf,fd->gtd', activated, narrow_weight, precision=HIGHEST) + narrow_bias)

def forward(params, stream, lengths):
    for which_layer in range(LAYERS):
        stream = residual_block(params, stream, lengths)
    places = jnp.arange(SEQ, dtype=jnp.int32)
    valid_mask = (places[None, :] < lengths[:, None]).astype(stream.dtype)
    return stream * valid_mask[:, :, None]

def reference(tokens, lengths, entry_gain, entry_shift, joined_weight, joined_bias, mixer_weight, mixer_bias, middle_gain, middle_shift, widen_weight, widen_bias, narrow_weight, narrow_bias, cotangent):
    params = tuple((weight.astype(jnp.float32) for weight in (entry_gain, entry_shift, joined_weight, joined_bias, mixer_weight, mixer_bias, middle_gain, middle_shift, widen_weight, widen_bias, narrow_weight, narrow_bias)))
    groups = BATCH // SEQS_DEV
    streams = tokens.astype(jnp.float32).reshape(groups, SEQS_DEV, SEQ, D)
    spans = lengths.reshape(groups, SEQS_DEV)
    tangents = cotangent.astype(jnp.float32).reshape(groups, SEQS_DEV, SEQ, D)

    def one_group(totals, inputs):
        stream, span_group, tangent = inputs

        def closed(weights, entries):
            return forward(weights, entries, span_group)
        result, pullback = jax.vjp(closed, params, stream)
        weight_grads, entry_grad = pullback(tangent)
        totals = jax.tree.map(jnp.add, totals, weight_grads)
        return (totals, (result, entry_grad))
    zero_grads = jax.tree.map(jnp.zeros_like, params)
    totals, (results, entry_grads) = lax.scan(one_group, zero_grads, (streams, spans, tangents))
    mixed_out = results.reshape(BATCH, SEQ, D).astype(jnp.bfloat16)
    tokens_grad = entry_grads.reshape(BATCH, SEQ, D).astype(jnp.bfloat16)
    entry_gain_grad, entry_shift_grad, joined_weight_grad, joined_bias_grad, mixer_weight_grad, mixer_bias_grad, middle_gain_grad, middle_shift_grad, widen_weight_grad, widen_bias_grad, narrow_weight_grad, narrow_bias_grad = tuple((total.astype(jnp.float32) for total in totals))
    return (mixed_out, tokens_grad, entry_gain_grad, entry_shift_grad, joined_weight_grad, joined_bias_grad, mixer_weight_grad, mixer_bias_grad, middle_gain_grad, middle_shift_grad, widen_weight_grad, widen_bias_grad, narrow_weight_grad, narrow_bias_grad)
```

```python
import functools

import jax
import jax.numpy as jnp
from jax import lax
from jax.experimental import pallas as pl
from jax.experimental.pallas import tpu as pltpu
from jax.sharding import PartitionSpec as P

HD = 64
LAYERS = 2
EPSILON = 1e-05
NEGATIVE = -1e30
f32 = jnp.float32
bf16 = jnp.bfloat16
NN = ((1,), (0,))
NT = ((1,), (1,))
TN = ((0,), (0,))
TT = ((0,), (1,))


def dot(left, right, dims):
    return lax.dot_general(left, right, (dims, ((), ())), preferred_element_type=f32)


def layer_norm(inputs, gain_row, shift_row):
    center = jnp.mean(inputs, axis=-1, keepdims=True)
    offset = inputs - center
    spread = jnp.mean(offset * offset, axis=-1, keepdims=True)
    return offset * lax.rsqrt(spread + EPSILON) * gain_row + shift_row


def gelu_tanh(values):
    return jax.nn.gelu(values, approximate=True)


def causal_mask(first, rows, length):
    keys = lax.broadcasted_iota(jnp.int32, (rows, rows), 0)
    queries = lax.broadcasted_iota(jnp.int32, (rows, rows), 1)
    return (keys <= queries) & (keys + first < length)


def attend_forward_body(n, rows, len_ref, q_ref, k_ref, v_ref, o_ref, l_ref):
    length = len_ref[pl.program_id(0)]
    hd = q_ref.shape[3]
    keys = [k_ref[j, 0, 0].T for j in range(n)]
    for i in range(n):

        @pl.when(i * rows < length)
        def _():
            query = q_ref[i, 0, 0] * jnp.asarray(hd**-0.5, bf16)
            scores = []
            for j in range(i + 1):
                block = dot(keys[j], query, NN)
                if j == i:
                    block = jnp.where(causal_mask(j * rows, rows, length), block, NEGATIVE)
                scores.append(block)
            top = scores[0].max(axis=0, keepdims=True)
            for j in range(1, i + 1):
                top = jnp.maximum(top, scores[j].max(axis=0, keepdims=True))
            total = jnp.zeros((1, rows), f32)
            out = jnp.zeros((hd, rows), f32)
            for j in range(i + 1):
                lifted = jnp.exp(scores[j] - top)
                total = total + lifted.sum(axis=0, keepdims=True)
                out = out + dot(v_ref[j, 0, 0], lifted.astype(bf16), NN)
            o_ref[i, 0] = (out / total).astype(bf16)
            l_ref[0, 0, i : i + 1, :] = top + jnp.log(total)

        @pl.when(i * rows >= length)
        def _():
            o_ref[i, 0] = jnp.zeros((hd, rows), bf16)
            l_ref[0, 0, i : i + 1, :] = jnp.zeros((1, rows), f32)


def attend_backward_body(
    n, rows, len_ref, q_ref, k_ref, v_ref, g_ref, o_ref, l_ref, d_ref, dk_acc, dv_acc
):
    length = len_ref[pl.program_id(0)]
    hd = q_ref.shape[3]
    keys = [k_ref[j, 0, 0].T for j in range(n)]
    vals = [v_ref[j, 0, 0].T for j in range(n)]
    dk_acc[...] = jnp.zeros_like(dk_acc)
    dv_acc[...] = jnp.zeros_like(dv_acc)
    for i in range(n):

        @pl.when(i * rows < length)
        def _():
            query = q_ref[i, 0, 0]
            scaled = query * jnp.asarray(hd**-0.5, bf16)
            grad = g_ref[i, 0]
            scaled_rows = scaled.T
            grad_rows = grad.T
            logsum = l_ref[0, 0, i : i + 1, :]
            centre = (grad.astype(f32) * o_ref[i, 0].astype(f32)).sum(axis=0, keepdims=True)
            dq = jnp.zeros((hd, rows), f32)
            for j in range(i + 1):
                share = jnp.exp(dot(keys[j], scaled, NN) - logsum)
                if j == i:
                    share = jnp.where(causal_mask(j * rows, rows, length), share, 0.0)
                share_grad = dot(vals[j], grad, NN)
                score_grad = (share * (share_grad - centre)).astype(bf16)
                dv_acc[j] += dot(share.astype(bf16), grad_rows, NN)
                dk_acc[j] += dot(score_grad, scaled_rows, NN)
                dq = dq + dot(k_ref[j, 0, 0], score_grad, NN)
            d_ref[i, 0, 0] = (dq * (hd**-0.5)).astype(bf16)

        @pl.when(i * rows >= length)
        def _():
            d_ref[i, 0, 0] = jnp.zeros((hd, rows), bf16)

    for j in range(n):
        d_ref[j, 1, 0] = dk_acc[j].astype(bf16).T
        d_ref[j, 2, 0] = dv_acc[j].astype(bf16).T


def attention_specs(packed, seqs):
    n, _, heads, hd, cols = packed.shape
    rows = cols // seqs

    def part(which):
        return pl.BlockSpec((n, 1, 1, hd, rows), lambda b, h, L: (0, which, h, 0, b))

    item = pl.BlockSpec((n, 1, hd, rows), lambda b, h, L: (0, h, 0, b))
    line = pl.BlockSpec((1, 1, n, rows), lambda b, h, L: (b, h, 0, 0))
    return n, heads, hd, cols, rows, part, item, line


def attend_forward(packed, lengths):
    seqs = lengths.shape[0]
    n, heads, hd, cols, rows, part, item, line = attention_specs(packed, seqs)
    blocks = seqs * heads * n * (n + 1) // 2
    return pl.pallas_call(
        functools.partial(attend_forward_body, n, rows),
        grid_spec=pltpu.PrefetchScalarGridSpec(
            num_scalar_prefetch=1,
            grid=(seqs, heads),
            in_specs=[part(0), part(1), part(2)],
            out_specs=[item, line],
        ),
        out_shape=[
            jax.ShapeDtypeStruct((n, heads, hd, cols), bf16),
            jax.ShapeDtypeStruct((seqs, heads, n, rows), f32),
        ],
        cost_estimate=pl.CostEstimate(
            flops=4 * blocks * rows * rows * hd,
            bytes_accessed=4 * n * heads * hd * cols * 2,
            transcendentals=blocks * rows * rows,
        ),
        name="attend_forward",
    )(lengths, packed, packed, packed)


def attend_backward(packed, grad, out, logsum, lengths):
    seqs = lengths.shape[0]
    n, heads, hd, cols, rows, part, item, line = attention_specs(packed, seqs)
    blocks = seqs * heads * n * (n + 1) // 2
    return pl.pallas_call(
        functools.partial(attend_backward_body, n, rows),
        grid_spec=pltpu.PrefetchScalarGridSpec(
            num_scalar_prefetch=1,
            grid=(seqs, heads),
            in_specs=[part(0), part(1), part(2), item, item, line],
            out_specs=pl.BlockSpec((n, 3, 1, hd, rows), lambda b, h, L: (0, 0, h, 0, b)),
            scratch_shapes=[pltpu.VMEM((n, rows, hd), f32), pltpu.VMEM((n, rows, hd), f32)],
        ),
        out_shape=jax.ShapeDtypeStruct((n, 3, heads, hd, cols), bf16),
        cost_estimate=pl.CostEstimate(
            flops=10 * blocks * rows * rows * hd,
            bytes_accessed=8 * n * heads * hd * cols * 2,
            transcendentals=blocks * rows * rows,
        ),
        name="attend_backward",
    )(lengths, packed, packed, packed, grad, out, logsum)


def forward_layer(stream, gathered, lengths, seq_count):
    (
        entry_gain,
        entry_shift,
        joined_weight,
        joined_bias,
        mixer_weight,
        mixer_bias,
        middle_gain,
        middle_shift,
        widen_weight,
        widen_bias,
        narrow_weight,
        narrow_bias,
    ) = gathered
    features = stream.shape[1]
    local_rows = stream.shape[0] // seq_count
    normed = layer_norm(
        stream, entry_gain.astype(jnp.float32), entry_shift.astype(jnp.float32)
    ).astype(jnp.bfloat16)
    groups = lax.axis_size("seq")
    bias_row = jnp.concatenate(
        [joined_bias[:features], jnp.zeros((features,), jnp.bfloat16), joined_bias[features:]]
    ).astype(jnp.float32)
    bias_row = bias_row.reshape(3, groups, features // groups).transpose(1, 0, 2).reshape(-1, 1)
    joined_rows = (dot(joined_weight, normed, TT) + bias_row).astype(jnp.bfloat16)
    heads_here = features // groups // HD
    packed = swap_groups(joined_rows.reshape(groups, 3, heads_here, HD, stream.shape[0]))
    mixed, logsum = attend_forward(packed, lengths)
    attended = swap_groups(mixed).reshape(features, stream.shape[0])
    middle = (
        stream
        + dot(attended, mixer_weight, TN)
        + mixer_bias.astype(jnp.float32)
    )
    normed_two = layer_norm(
        middle, middle_gain.astype(jnp.float32), middle_shift.astype(jnp.float32)
    ).astype(jnp.bfloat16)
    widened = jnp.dot(
        normed_two, widen_weight, preferred_element_type=jnp.float32
    ) + widen_bias.astype(jnp.float32)
    activated = gelu_tanh(widened).astype(jnp.bfloat16)
    output = (
        middle
        + jnp.dot(activated, narrow_weight, preferred_element_type=jnp.float32)
        + narrow_bias.astype(jnp.float32)
    )
    saved = (
        stream,
        normed,
        packed,
        mixed,
        logsum,
        attended,
        middle,
        normed_two,
        widened,
        activated,
    )
    return (output, saved)


def backward_layer(upstream, saved, gathered, lengths, seq_count):
    (
        entry_gain,
        entry_shift,
        joined_weight,
        joined_bias,
        mixer_weight,
        mixer_bias,
        middle_gain,
        middle_shift,
        widen_weight,
        widen_bias,
        narrow_weight,
        narrow_bias,
    ) = gathered
    (
        stream,
        normed,
        packed,
        mixed,
        logsum,
        attended,
        middle,
        normed_two,
        widened,
        activated,
    ) = saved
    features = stream.shape[1]
    local_rows = stream.shape[0] // seq_count
    branch_grad = upstream.astype(jnp.bfloat16)
    narrow_weight_term = jnp.einsum(
        "tf,td->fd", activated, branch_grad, preferred_element_type=jnp.float32
    )
    narrow_bias_term = jnp.sum(branch_grad.astype(jnp.float32), axis=0)
    activated_grad = jnp.einsum(
        "td,fd->tf", branch_grad, narrow_weight, preferred_element_type=jnp.float32
    )
    widened_grad = jax.vjp(gelu_tanh, widened)[1](activated_grad)[0].astype(jnp.bfloat16)
    widen_weight_term = jnp.einsum(
        "td,tf->df", normed_two, widened_grad, preferred_element_type=jnp.float32
    )
    widen_bias_term = jnp.sum(widened_grad.astype(jnp.float32), axis=0)
    normed_two_grad = jnp.einsum(
        "tf,df->td", widened_grad, widen_weight, preferred_element_type=jnp.float32
    )
    middle_pull = jax.vjp(
        layer_norm, middle, middle_gain.astype(jnp.float32), middle_shift.astype(jnp.float32)
    )[1]
    middle_grad, middle_gain_term, middle_shift_term = middle_pull(normed_two_grad)
    middle_grad = middle_grad + upstream
    mixer_grad = middle_grad.astype(jnp.bfloat16)
    mixer_weight_term = dot(attended, mixer_grad, NN)
    mixer_bias_term = jnp.sum(mixer_grad.astype(jnp.float32), axis=0)
    attended_grad = dot(mixer_weight, mixer_grad, NT).astype(jnp.bfloat16)
    groups = lax.axis_size("seq")
    heads_grad = swap_groups(attended_grad.reshape(mixed.shape))
    packed_grad = attend_backward(packed, heads_grad, mixed, logsum, lengths)
    joined_grad = swap_groups(packed_grad).reshape(3 * features, stream.shape[0])
    joined_weight_term = dot(normed, joined_grad, TT)
    joined_sums = jnp.sum(joined_grad.astype(jnp.float32), axis=1)
    joined_sums = (
        joined_sums.reshape(groups, 3, features // groups).transpose(1, 0, 2).reshape(3, features)
    )
    joined_bias_term = jnp.concatenate([joined_sums[0], joined_sums[2]])
    normed_grad = dot(joined_grad, joined_weight, TT)
    entry_pull = jax.vjp(
        layer_norm, stream, entry_gain.astype(jnp.float32), entry_shift.astype(jnp.float32)
    )[1]
    stream_grad, entry_gain_term, entry_shift_term = entry_pull(normed_grad)
    stream_grad = stream_grad + middle_grad
    grad_terms = (
        entry_gain_term,
        entry_shift_term,
        joined_weight_term,
        joined_bias_term,
        mixer_weight_term,
        mixer_bias_term,
        middle_gain_term,
        middle_shift_term,
        widen_weight_term,
        widen_bias_term,
        narrow_weight_term,
        narrow_bias_term,
    )
    return (stream_grad, grad_terms)


def swap_groups(blocks):
    return lax.all_to_all(blocks, "seq", split_axis=0, concat_axis=0, tiled=True)


def local(
    tokens,
    lengths,
    entry_gain,
    entry_shift,
    joined_weight,
    joined_bias,
    mixer_weight,
    mixer_bias,
    middle_gain,
    middle_shift,
    widen_weight,
    widen_bias,
    narrow_weight,
    narrow_bias,
    cotangent,
):
    groups = lax.axis_size("seq")
    rows_here = joined_weight.shape[0]
    joined_weight = (
        joined_weight.reshape(rows_here, 3, groups, -1).transpose(0, 2, 1, 3).reshape(rows_here, -1)
    )
    gathered = (
        lax.all_gather(entry_gain, ("dp", "seq"), axis=0, tiled=True),
        lax.all_gather(entry_shift, ("dp", "seq"), axis=0, tiled=True),
        lax.all_gather(joined_weight, ("dp", "seq"), axis=0, tiled=True),
        lax.all_gather(joined_bias, ("dp", "seq"), axis=0, tiled=True),
        lax.all_gather(mixer_weight, ("dp", "seq"), axis=0, tiled=True),
        lax.all_gather(mixer_bias, ("dp", "seq"), axis=0, tiled=True),
        lax.all_gather(middle_gain, ("dp", "seq"), axis=0, tiled=True),
        lax.all_gather(middle_shift, ("dp", "seq"), axis=0, tiled=True),
        lax.all_gather(widen_weight, ("dp", "seq"), axis=0, tiled=True),
        lax.all_gather(widen_bias, ("dp", "seq"), axis=0, tiled=True),
        lax.all_gather(narrow_weight, ("dp", "seq"), axis=0, tiled=True),
        lax.all_gather(narrow_bias, ("dp", "seq"), axis=0, tiled=True),
    )
    seq_count, local_rows, features = tokens.shape
    places = lax.axis_index("seq") * local_rows + jnp.arange(local_rows, dtype=jnp.int32)
    valid_mask = (
        (places[None, :] < lengths[:, None]).astype(jnp.float32).reshape(seq_count * local_rows, 1)
    )
    stream = tokens.astype(jnp.float32).reshape(seq_count * local_rows, features)
    saved_layers = []
    for which_layer in range(LAYERS):
        stream, saved = forward_layer(stream, gathered, lengths, seq_count)
        saved_layers.append(saved)
    mixed_out = (stream * valid_mask).astype(jnp.bfloat16).reshape(seq_count, local_rows, features)
    upstream = cotangent.astype(jnp.float32).reshape(seq_count * local_rows, features) * valid_mask
    gathered = (
        lax.all_gather(entry_gain, ("dp", "seq"), axis=0, tiled=True),
        lax.all_gather(entry_shift, ("dp", "seq"), axis=0, tiled=True),
        lax.all_gather(joined_weight, ("dp", "seq"), axis=0, tiled=True),
        lax.all_gather(joined_bias, ("dp", "seq"), axis=0, tiled=True),
        lax.all_gather(mixer_weight, ("dp", "seq"), axis=0, tiled=True),
        lax.all_gather(mixer_bias, ("dp", "seq"), axis=0, tiled=True),
        lax.all_gather(middle_gain, ("dp", "seq"), axis=0, tiled=True),
        lax.all_gather(middle_shift, ("dp", "seq"), axis=0, tiled=True),
        lax.all_gather(widen_weight, ("dp", "seq"), axis=0, tiled=True),
        lax.all_gather(widen_bias, ("dp", "seq"), axis=0, tiled=True),
        lax.all_gather(narrow_weight, ("dp", "seq"), axis=0, tiled=True),
        lax.all_gather(narrow_bias, ("dp", "seq"), axis=0, tiled=True),
    )
    shard_list = (
        entry_gain,
        entry_shift,
        joined_weight,
        joined_bias,
        mixer_weight,
        mixer_bias,
        middle_gain,
        middle_shift,
        widen_weight,
        widen_bias,
        narrow_weight,
        narrow_bias,
    )
    totals = tuple((jnp.zeros(one_shard.shape, jnp.float32) for one_shard in shard_list))
    for which_layer in reversed(range(LAYERS)):
        upstream, grad_terms = backward_layer(
            upstream, saved_layers[which_layer], gathered, lengths, seq_count
        )
        grad_terms = (
            lax.psum_scatter(grad_terms[0], ("dp", "seq"), scatter_dimension=0, tiled=True),
            lax.psum_scatter(grad_terms[1], ("dp", "seq"), scatter_dimension=0, tiled=True),
            lax.psum_scatter(grad_terms[2], ("dp", "seq"), scatter_dimension=0, tiled=True),
            lax.psum_scatter(grad_terms[3], ("dp", "seq"), scatter_dimension=0, tiled=True),
            lax.psum_scatter(grad_terms[4], ("dp", "seq"), scatter_dimension=0, tiled=True),
            lax.psum_scatter(grad_terms[5], ("dp", "seq"), scatter_dimension=0, tiled=True),
            lax.psum_scatter(grad_terms[6], ("dp", "seq"), scatter_dimension=0, tiled=True),
            lax.psum_scatter(grad_terms[7], ("dp", "seq"), scatter_dimension=0, tiled=True),
            lax.psum_scatter(grad_terms[8], ("dp", "seq"), scatter_dimension=0, tiled=True),
            lax.psum_scatter(grad_terms[9], ("dp", "seq"), scatter_dimension=0, tiled=True),
            lax.psum_scatter(grad_terms[10], ("dp", "seq"), scatter_dimension=0, tiled=True),
            lax.psum_scatter(grad_terms[11], ("dp", "seq"), scatter_dimension=0, tiled=True),
        )
        totals = tuple((left + right for left, right in zip(totals, grad_terms)))
    totals = list(totals)
    totals[2] = (
        totals[2].reshape(rows_here, groups, 3, -1).transpose(0, 2, 1, 3).reshape(rows_here, -1)
    )
    tokens_grad = upstream.astype(jnp.bfloat16).reshape(seq_count, local_rows, features)
    return (
        mixed_out,
        tokens_grad,
        totals[0],
        totals[1],
        totals[2],
        totals[3],
        totals[4],
        totals[5],
        totals[6],
        totals[7],
        totals[8],
        totals[9],
        totals[10],
        totals[11],
    )


def solution(mesh):
    return jax.shard_map(
        local,
        mesh=mesh,
        in_specs=(
            P("dp", "seq", None),
            P("dp"),
            P(("dp", "seq")),
            P(("dp", "seq")),
            P(("dp", "seq"), None),
            P(("dp", "seq")),
            P(("dp", "seq"), None),
            P(("dp", "seq")),
            P(("dp", "seq")),
            P(("dp", "seq")),
            P(("dp", "seq"), None),
            P(("dp", "seq")),
            P(("dp", "seq"), None),
            P(("dp", "seq")),
            P("dp", "seq", None),
        ),
        out_specs=(
            P("dp", "seq", None),
            P("dp", "seq", None),
            P(("dp", "seq")),
            P(("dp", "seq")),
            P(("dp", "seq"), None),
            P(("dp", "seq")),
            P(("dp", "seq"), None),
            P(("dp", "seq")),
            P(("dp", "seq")),
            P(("dp", "seq")),
            P(("dp", "seq"), None),
            P(("dp", "seq")),
            P(("dp", "seq"), None),
            P(("dp", "seq")),
        ),
        check_vma=False,
    )
```
